128 devices in a mesh: sector: 8 (over y, core), term: 16 (over x, z).
Axes of the slice: x: 4, y: 4, z: 4, core: 2. Of those that a mesh axis runs over, the one named last changes fastest.
Arguments:
- trial: float32 [16, 512, 512], P('sector', 'term'), may hold values from -6 to 6
- precond: float32 [16, 512, 512], P('sector', 'term'), may hold values from 2 to 16
- sector_dims: int32 [16], P('sector'), may hold values from 128 to 512
- left_ops: float32 [1024, 512, 512], P(('sector', 'term')), may hold values from -0.25 to 0.25
- right_ops: float32 [1024, 512, 512], P(('sector', 'term')), may hold values from -0.25 to 0.25
- task_source: int32 [1024], P(('sector', 'term')), may hold values from 0 to 1
- task_target: int32 [1024], P(('sector', 'term')), may hold values from 0 to 1
- task_count: int32 [128], P(('sector', 'term')), may hold values from 1 to 7, as said below
Outputs:
- trial_out: float32 [16, 512, 512], P('sector', 'term')
- ritz: float32 [3], replicated
The draws below stay inside these ranges and needn't reach their ends.
Inputs may be any that keep to these rules, and one draw needn't show every extreme that they name: `task_count`: the counts of two devices with the same sector index whose term indices differ by half the term axis add up to 8.
All inputs are finite; a program needn't handle non-finite values.
Results may differ from the reference program's by a relative error of at most 0.0003.
Values sent between devices are 32-bit elements; how exact they have to be, the bound alone decides.
A program may use at most 64 MiB of HBM per device.

```python
import math
import jax
import jax.numpy as jnp
from jax import lax

B = 512
SEC_DEV = 2
CAP = 8
STEPS = 3
SECTORS = 16
SLOTS = 1024
N_TERM = 16
DEVICES = 128


def draw_sector_dims(key, part):
    values = jax.random.randint(jax.random.fold_in(key, 11), (SECTORS,), B // 4, B + 1, dtype=jnp.int32)
    index = jnp.arange(SECTORS, dtype=jnp.int32)
    return jnp.where(index == 0, B, values)


def draw_task_count(key, part):
    values = jax.random.randint(jax.random.fold_in(key, 23), (DEVICES,), 1, CAP, dtype=jnp.int32)
    index = jnp.arange(DEVICES, dtype=jnp.int32)
    values = jnp.where(index == 0, CAP - 1, values)
    half = N_TERM // 2
    lower = index % N_TERM < half
    partner = jnp.where(lower, index, index - half)
    paired = values[partner]
    return jnp.where(lower, paired, CAP - paired)


def with_ends(array, own_key, low, top_value):
    longest = array.shape.index(max(array.shape))
    spots = []
    for shift in (0, 1):
        where = [jax.random.randint(jax.random.fold_in(own_key, axis), (), 0, length) for axis, length in enumerate(array.shape)]
        where[longest] = (where[longest] + shift) % array.shape[longest]
        spots.append(tuple(where))
    return array.at[spots[0]].set(low).at[spots[1]].set(top_value)


def block_scale(rng, dims, shards, low, high):
    def one(dim, shards_of):
        steps = jax.random.uniform(jax.random.fold_in(jax.random.fold_in(rng, 6), dim), (shards_of,), jnp.float32, low / len(shards), high / len(shards))
        return jnp.repeat(jnp.exp(steps), dims[dim] // shards_of).reshape((-1,) + (1,) * (len(dims) - dim - 1))

    factor_of = one(*shards[0])
    for cut in shards[1:]:
        factor_of = factor_of * one(*cut)
    return factor_of


def scatter_about(own_key, shape, deviation, reach, split=(), kind=jnp.bfloat16):
    values = deviation * jax.random.normal(own_key, shape, jnp.float32)
    if split:
        values = values * block_scale(own_key, shape, split, -0.22, 0.18)
    return jnp.clip(values, -reach, reach).astype(kind)


def setup_inputs(seed: int = 0) -> dict:
    streams_of = jax.random.split(jax.random.key(seed), 9)
    return {
        "trial": scatter_about(streams_of[0], (SECTORS, B, B), 1.0, 6.0, ((0, 8), (1, 16)), jnp.float32),
        "precond": jnp.clip(jnp.exp(math.log(16.0) - 2.0794415 * jax.random.uniform(streams_of[1], (SECTORS, B, B), jnp.float32) ** block_scale(streams_of[1], (SECTORS, B, B), ((0, 8), (1, 16)), -0.2, 0.2)), 2.0, 16.0),
        "sector_dims": draw_sector_dims(jax.random.fold_in(streams_of[8], 71), 0),
        "left_ops": scatter_about(streams_of[3], (SLOTS, B, B), B ** -0.5, 0.25, ((0, 128),), jnp.float32),
        "right_ops": scatter_about(streams_of[4], (SLOTS, B, B), B ** -0.5, 0.25, ((0, 128),), jnp.float32),
        "task_source": with_ends(jax.random.randint(streams_of[5], (SLOTS,), 0, SEC_DEV), jax.random.fold_in(streams_of[5], 1), 0, SEC_DEV - 1).astype(jnp.int32),
        "task_target": with_ends(jax.random.randint(streams_of[6], (SLOTS,), 0, SEC_DEV), jax.random.fold_in(streams_of[6], 1), 0, SEC_DEV - 1).astype(jnp.int32),
        "task_count": draw_task_count(jax.random.fold_in(streams_of[8], 71), 0),
    }


def reference(trial, precond, sector_dims, left_ops, right_ops, task_source, task_target, task_count):
    index = jnp.arange(B, dtype=jnp.int32)
    inside = index[None, :] < sector_dims[:, None]
    mask = (inside[:, :, None] & inside[:, None, :]).astype(trial.dtype)
    cells = SECTORS * B * B
    highest = lax.Precision.HIGHEST

    def rescale(u):
        return u * jnp.sqrt(cells / jnp.sum(u * u))

    def sigma_of(vector):

        def one(acc, items):
            left, right, source, target, slot = items
            device = slot // CAP
            group = device // N_TERM
            live = slot % CAP < task_count[device]
            src = (group * SEC_DEV + source).astype(jnp.int32)
            tgt = (group * SEC_DEV + target).astype(jnp.int32)

            def work(total):
                block = lax.dynamic_index_in_dim(vector, src, 0, keepdims=False)
                inner = jnp.dot(block, right, precision=highest)
                product = jnp.dot(left, inner, precision=highest)
                old = lax.dynamic_index_in_dim(total, tgt, 0, keepdims=True)
                return lax.dynamic_update_index_in_dim(total, old + product[None], tgt, 0)
            return (lax.cond(live, work, lambda total: total, acc), None)
        slots = jnp.arange(SLOTS, dtype=jnp.int32)
        acc, _ = lax.scan(one, jnp.zeros_like(vector), (left_ops, right_ops, task_source, task_target, slots))
        return acc * mask
    vector = rescale(mask * trial)
    values = []
    for step in range(STEPS):
        sig = sigma_of(vector)
        theta = jnp.sum(vector * sig) / jnp.sum(vector * vector)
        values.append(theta)
        vector = rescale(vector - (sig - theta * vector) / precond)
    return (vector, jnp.stack(values))
```

```python
import functools

import jax
import jax.numpy as jnp
from jax import lax
from jax.experimental import pallas as pl
from jax.experimental.pallas import tpu as pltpu
from jax.sharding import Mesh
from jax.sharding import PartitionSpec as P

STEPS = 3
LIVE = 7
SECTOR = ("sector_0", "sector_1")
TERM = ("term_0", "term_1")
SECTOR_TERM = SECTOR + TERM
MESH = pl.DeviceIdType.MESH
F32 = jnp.float32
BF16 = jnp.bfloat16


def halves(x):
    hi = x.astype(BF16)
    return hi, (x - hi.astype(F32)).astype(BF16)


def product(a_hi, a_lo, b_hi, b_lo):
    dot = functools.partial(jnp.dot, preferred_element_type=F32)
    return dot(a_hi, b_hi) + dot(a_hi, b_lo) + dot(a_lo, b_hi)


def kernel(
    cells,
    groups,
    trial,
    precond,
    dims,
    source,
    target,
    count,
    left_ops,
    right_ops,
    out,
    ritz,
    vec,
    vec_hi,
    vec_lo,
    part,
    in_f1,
    in_f2,
    in_g1,
    in_g2,
    stage_l,
    stage_r,
    left_hi,
    left_lo,
    right_hi,
    right_lo,
    inner_hi,
    inner_lo,
    own_sums,
    term_sums,
    group_sums,
    sector_sums,
    ag_send,
    ag_recv,
    rs_send,
    f1_recv,
    f2_recv,
    g1_recv,
    g2_recv,
    sum_send,
    sum_recv,
    load_sem,
):
    n_y, n_c = groups
    y, core = lax.axis_index("sector_0"), lax.axis_index("sector_1")
    x, z = lax.axis_index("term_0"), lax.axis_index("term_1")
    slots = left_hi.shape[0]
    width = left_hi.shape[1]
    coords = ((x, z), (z, x))
    names = (("term_0", "term_1"), ("term_1", "term_0"))

    def up(a, by):
        return lax.rem(a + by, 4)

    def unit(c, dp, dq):
        p, q = coords[c]
        return up(p, dp) * 4 + up(q, dq)

    def beside(c, axis, way):
        return {names[c][axis]: up(coords[c][axis], 1 if way == 0 else 3)}

    def load(k, which):
        src, dst = ((right_ops, stage_r), (left_ops, stage_l))[which]
        return pltpu.make_async_copy(src.at[k], dst.at[k], load_sem.at[which, k])

    for which in range(2):
        for k in range(slots):
            load(k, which).start()

    barrier = pltpu.get_barrier_semaphore()
    for d in range(1, 16):
        there = lax.rem(x * 4 + z + d, 16)
        pl.semaphore_signal(
            barrier, inc=1, device_id={"term_0": there // 4, "term_1": lax.rem(there, 4)}, device_id_type=MESH
        )
    n_groups = n_y * n_c
    for d in range(1, n_groups):
        there = lax.rem(y * n_c + core + d, n_groups)
        pl.semaphore_signal(
            barrier, inc=1, device_id={"sector_0": there // n_c, "sector_1": lax.rem(there, n_c)}, device_id_type=MESH
        )

    def mask(c, s):
        row = (x * 4 + z) * 32 + c * 16 + lax.broadcasted_iota(jnp.int32, (16, width), 0)
        col = lax.broadcasted_iota(jnp.int32, (16, width), 1)
        return (row < dims[s]) & (col < dims[s])

    for c in range(2):
        for s in range(2):
            vec[c, unit(c, 0, 0), s] = jnp.where(mask(c, s), trial[s, c * 16 : (c + 1) * 16], 0.0)

    pl.semaphore_wait(barrier, 15 + n_groups - 1)

    def remote(src, dst, send, recv, where):
        return pltpu.make_async_remote_copy(
            src_ref=src, dst_ref=dst, send_sem=send, recv_sem=recv, device_id=where, device_id_type=MESH
        )

    def ag_full(c, line, way, at):
        ref = vec.at[c, at]
        return remote(ref, ref, ag_send, ag_recv.at[c, line, way], beside(c, 0 if line else 1, way))

    def ag_half(c, line, way, at):
        ref = vec.at[c, at, way]
        return remote(ref, ref, ag_send, ag_recv.at[c, line, 2 + way], beside(c, 0 if line else 1, way))

    def lane_sums(value):
        folded = jnp.sum(value.reshape(-1, width), axis=0, keepdims=True)
        total = folded[:, 0:128]
        for i in range(1, width // 128):
            total = total + folded[:, i * 128 : (i + 1) * 128]
        return total

    def squares():
        total = jnp.zeros((1, 128), F32)
        for c in range(2):
            value = vec[c, unit(c, 0, 0)]
            total = total + lane_sums(value * value)
        return total

    def term_start(step):
        for d in range(1, 16):
            there = lax.rem(x * 4 + z + d, 16)
            remote(
                own_sums.at[step],
                term_sums.at[step, x * 4 + z],
                sum_send.at[step, 0],
                sum_recv.at[step, 0],
                {"term_0": there // 4, "term_1": lax.rem(there, 4)},
            ).start()
        term_sums[step, x * 4 + z] = own_sums[step]

    def wait_bytes(ref, sem):
        pltpu.make_async_copy(ref, ref, sem).wait()

    def sector_start(step):
        wait_bytes(term_sums.at[step, 0:15], sum_recv.at[step, 0])
        group_sums[step] = jnp.sum(term_sums[step], axis=0)
        me = y * n_c + core
        for d in range(1, n_groups):
            there = lax.rem(me + d, n_groups)
            remote(
                group_sums.at[step],
                sector_sums.at[step, me],
                sum_send.at[step, 1],
                sum_recv.at[step, 1],
                {"sector_0": there // n_c, "sector_1": lax.rem(there, n_c)},
            ).start()
        sector_sums[step, me] = group_sums[step]

    def sums_end(step):
        if n_groups > 1:
            wait_bytes(sector_sums.at[step, 0 : n_groups - 1], sum_recv.at[step, 1])
        total = jnp.sum(jnp.sum(sector_sums[step], axis=0), axis=1, keepdims=True)
        wait_bytes(term_sums.at[step, 0:15], sum_send.at[step, 0])
        if n_groups > 1:
            wait_bytes(sector_sums.at[step, 0 : n_groups - 1], sum_send.at[step, 1])
        return total

    def prepare(which):
        stage, hi, lo = ((stage_r, right_hi, right_lo), (stage_l, left_hi, left_lo))[which]
        for k in range(slots):
            load(k, which).wait()

        def body(i, carry):
            k = i // 8
            rows = pl.ds(pl.multiple_of(lax.rem(i, 8) * (width // 8), width // 8), width // 8)
            hi[k, rows], lo[k, rows] = halves(stage[k, rows])
            return carry

        lax.fori_loop(0, slots * 8, body, 0)

    def offsets(block):
        px, pz = up(x, block), up(z, block)
        first = [pl.multiple_of(px * 128 + i * 32, 32) for i in range(4)]
        second = [pl.multiple_of(i * 128 + pz * 32 + 16, 16) for i in range(4)]
        return first + second

    def units(c, block):
        return pl.ds(up(coords[c][0], block) * 4, 4)

    def first_products(block):
        for c in range(2):
            for s in range(2):
                vec_hi[s, c, units(c, block)], vec_lo[s, c, units(c, block)] = halves(vec[c, units(c, block), s])
        offs = offsets(block)

        def body(k, carry):
            s = source[k]
            a_hi = jnp.concatenate([vec_hi[s, c, units(c, block)].reshape(64, width) for c in range(2)], axis=0)
            a_lo = jnp.concatenate([vec_lo[s, c, units(c, block)].reshape(64, width) for c in range(2)], axis=0)
            inner = product(a_hi, a_lo, right_hi[k], right_lo[k])
            hi, lo = halves(inner)
            for i, off in enumerate(offs):
                inner_hi[k, pl.ds(off, 16)] = hi[i * 16 : (i + 1) * 16]
                inner_lo[k, pl.ds(off, 16)] = lo[i * 16 : (i + 1) * 16]
            return carry

        lax.fori_loop(0, slots, body, 0)

    def second_products(block):
        offs = offsets(block)
        for c in range(2):
            part[c, units(c, block)] = jnp.zeros((4, 2, 16, width), F32)

        def body(k, carry):
            a_hi = jnp.concatenate([left_hi[k, pl.ds(off, 16)] for off in offs], axis=0)
            a_lo = jnp.concatenate([left_lo[k, pl.ds(off, 16)] for off in offs], axis=0)
            value = product(a_hi, a_lo, inner_hi[k], inner_lo[k])
            live = jnp.where(k < count[0], 1.0, 0.0).astype(F32)
            to_one = live * target[k].astype(F32)
            scale = (live - to_one, to_one)
            for c in range(2):
                piece = value[c * 64 : (c + 1) * 64].reshape(4, 16, width)
                for s in range(2):
                    part[c, units(c, block), s] = part[c, units(c, block), s] + scale[s] * piece
            return carry

        lax.fori_loop(0, slots, body, 0)
        total = jnp.zeros((1, 128), F32)
        for c in range(2):
            for i in range(4):
                at = up(coords[c][0], block) * 4 + i
                total = total + lane_sums(vec[c, at] * part[c, at])
        return total

    def f1(c, dq, way):
        return remote(
            part.at[c, unit(c, 2, dq), way],
            in_f1.at[c, dq, way],
            rs_send,
            f1_recv.at[c, dq, way],
            beside(c, 0, way),
        )

    def f2(c, dq, way):
        return remote(
            part.at[c, unit(c, 1 if way == 0 else 3, dq)],
            in_f2.at[c, dq, way],
            rs_send,
            f2_recv.at[c, dq, way],
            beside(c, 0, way),
        )

    def g1(c, way):
        return remote(
            part.at[c, unit(c, 0, 2), way], in_g1.at[c, way], rs_send, g1_recv.at[c, way], beside(c, 1, way)
        )

    def g2(c, way):
        return remote(
            part.at[c, unit(c, 0, 1 if way == 0 else 3)],
            in_g2.at[c, way],
            rs_send,
            g2_recv.at[c, way],
            beside(c, 1, way),
        )

    def one_step(step, carry):
        for c in range(2):
            for way in range(2):
                ag_full(c, 0, way, unit(c, 0, 0)).start()
        for c in range(2):
            for way in range(2):
                ag_full(c, 1, way, unit(c, 0, 0)).start()

        @pl.when(step == 0)
        def _():
            prepare(0)

        own_sums[step, 1:2] = squares()
        for c in range(2):
            for way in range(2):
                dq = 3 if way == 0 else 1
                at = unit(c, 0, dq)
                ag_full(c, 0, way, at).wait_recv()
                ag_half(c, 0, way, at).start()
                for w in range(2):
                    ag_full(c, 1 + dq, w, at).start()
        for c in range(2):
            for way in range(2):
                at = unit(c, 3 if way == 0 else 1, 0)
                ag_full(c, 1, way, at).wait_recv()
                ag_half(c, 1, way, at).start()
        for c in range(2):
            at = unit(c, 0, 2)
            for way in range(2):
                ag_half(c, 0, way, at).wait_recv()
            for way in range(2):
                ag_full(c, 3, way, at).start()
        first_products(0)

        @pl.when(step == 0)
        def _():
            prepare(1)

        for dq in (1, 3, 2):
            for c in range(2):
                for way in range(2):
                    at = unit(c, 3 if way == 0 else 1, dq)
                    ag_full(c, 1 + dq, way, at).wait_recv()
                    ag_half(c, 1 + dq, way, at).start()
        first_products(1)
        first_products(3)
        for dq in range(4):
            for c in range(2):
                for way in range(2):
                    ag_half(c, 1 + dq, way, unit(c, 2, dq)).wait_recv()
        first_products(2)
        wait_bytes(vec.at[0, 0:15], ag_send)
        wait_bytes(vec.at[1, 0:15], ag_send)

        order = (2, 1, 3, 0)
        total = second_products(2)
        for dq in order:
            for c in range(2):
                for way in range(2):
                    f1(c, dq, way).start()
        total = total + second_products(1)
        total = total + second_products(3)
        for dq in order:
            for c in range(2):
                for way in range(2):
                    f1(c, dq, way).wait_recv()
                    at = unit(c, 1 if way == 0 else 3, dq)
                    part[c, at, way] = part[c, at, way] + in_f1[c, dq, way]
                    f2(c, dq, way).start()
        total = total + second_products(0)
        own_sums[step, 0:1] = total
        term_start(step)

        def take_f2(c, dq):
            at = unit(c, 0, dq)
            for way in range(2):
                f2(c, dq, way).wait_recv()
            part[c, at] = part[c, at] + (in_f2[c, dq, 0] + in_f2[c, dq, 1])

        for c in range(2):
            take_f2(c, 2)
            for way in range(2):
                g1(c, way).start()
        for c in range(2):
            take_f2(c, 1)
            take_f2(c, 3)
        for c in range(2):
            for way in range(2):
                g1(c, way).wait_recv()
                at = unit(c, 0, 1 if way == 0 else 3)
                part[c, at, way] = part[c, at, way] + in_g1[c, way]
                g2(c, way).start()
        sector_start(step)
        for c in range(2):
            take_f2(c, 0)
        for c in range(2):
            for way in range(2):
                g2(c, way).wait_recv()
        sums = sums_end(step)
        vw, vv = sums[0:1], sums[1:2]
        theta = vw / vv
        ritz[step] = theta[0, 0]
        scale = jnp.sqrt(cells / vv)
        for c in range(2):
            at = unit(c, 0, 0)
            for s in range(2):
                w = part[c, at, s] + (in_g2[c, 0, s] + in_g2[c, 1, s])
                w = jnp.where(mask(c, s), w, 0.0)
                v = vec[c, at, s]
                vec[c, at, s] = (v - (w - theta * v) / precond[s, c * 16 : (c + 1) * 16]) * scale
        wait_bytes(part.at[0, 0:15], rs_send)
        wait_bytes(part.at[1, 0:15], rs_send)
        return carry

    lax.fori_loop(0, STEPS, one_step, 0)
    own_sums[STEPS, 0:1] = squares()
    own_sums[STEPS, 1:2] = jnp.zeros((1, 128), F32)
    term_start(STEPS)
    sector_start(STEPS)
    norm = sums_end(STEPS)[0:1]
    scale = jnp.sqrt(cells / norm)
    for c in range(2):
        for s in range(2):
            out[s, c * 16 : (c + 1) * 16] = vec[c, unit(c, 0, 0), s] * scale


def per_device(trial, precond, sector_dims, left_ops, right_ops, task_source, task_target, task_count):
    sec_dev, share, width = trial.shape
    groups = (lax.axis_size("sector_0"), lax.axis_size("sector_1"))
    n_groups = groups[0] * groups[1]
    cells = float(sec_dev * n_groups * width * width)
    vmem = pl.BlockSpec(memory_space=pltpu.VMEM)
    smem = pl.BlockSpec(memory_space=pltpu.SMEM)
    anywhere = pl.BlockSpec(memory_space=pl.ANY)
    dma = pltpu.SemaphoreType.DMA
    ops = (LIVE, width, width)
    return pl.pallas_call(
        functools.partial(kernel, cells, groups),
        out_shape=(
            jax.ShapeDtypeStruct(trial.shape, F32),
            jax.ShapeDtypeStruct((STEPS,), F32),
        ),
        in_specs=[vmem, vmem, smem, smem, smem, smem, anywhere, anywhere],
        out_specs=(vmem, smem),
        scratch_shapes=[
            pltpu.VMEM((2, 16, 2, 16, width), F32),
            pltpu.VMEM((2, 2, 16, 16, width), BF16),
            pltpu.VMEM((2, 2, 16, 16, width), BF16),
            pltpu.VMEM((2, 16, 2, 16, width), F32),
            pltpu.VMEM((2, 4, 2, 16, width), F32),
            pltpu.VMEM((2, 4, 2, 2, 16, width), F32),
            pltpu.VMEM((2, 2, 16, width), F32),
            pltpu.VMEM((2, 2, 2, 16, width), F32),
            pltpu.VMEM(ops, F32),
            pltpu.VMEM(ops, F32),
            pltpu.VMEM(ops, BF16),
            pltpu.VMEM(ops, BF16),
            pltpu.VMEM(ops, BF16),
            pltpu.VMEM(ops, BF16),
            pltpu.VMEM(ops, BF16),
            pltpu.VMEM(ops, BF16),
            pltpu.VMEM((STEPS + 1, 2, 128), F32),
            pltpu.VMEM((STEPS + 1, 16, 2, 128), F32),
            pltpu.VMEM((STEPS + 1, 2, 128), F32),
            pltpu.VMEM((STEPS + 1, n_groups, 2, 128), F32),
            dma,
            dma((2, 5, 4)),
            dma,
            dma((2, 4, 2)),
            dma((2, 4, 2)),
            dma((2, 2)),
            dma((2, 2)),
            dma((STEPS + 1, 2)),
            dma((STEPS + 1, 2)),
            dma((2, LIVE)),
        ],
        compiler_params=pltpu.CompilerParams(
            collective_id=0, has_side_effects=True, vmem_limit_bytes=60 * 1024 * 1024
        ),
    )(trial, precond, sector_dims, task_source, task_target, task_count, left_ops, right_ops)


def solution(mesh):
    finer = Mesh(mesh.devices.reshape(4, 2, 4, 4), SECTOR_TERM)
    placed = (
        P(SECTOR, TERM, None),
        P(SECTOR, TERM, None),
        P(SECTOR),
        P(SECTOR_TERM, None, None),
        P(SECTOR_TERM, None, None),
        P(SECTOR_TERM),
        P(SECTOR_TERM),
        P(SECTOR_TERM),
    )
    return jax.shard_map(
        per_device,
        mesh=finer,
        in_specs=placed,
        out_specs=(P(SECTOR, TERM, None), P()),
        check_vma=False,
    )
```

```python
import functools

import jax
import jax.numpy as jnp
from jax import lax
from jax.experimental import pallas as pl
from jax.experimental.pallas import tpu as pltpu
from jax.sharding import Mesh
from jax.sharding import PartitionSpec as P

STEPS = 3
LIVE = 7
SECTOR = ("sector_0", "sector_1")
TERM = ("term_0", "term_1")
SECTOR_TERM = SECTOR + TERM
MESH = pl.DeviceIdType.MESH
F32 = jnp.float32
BF16 = jnp.bfloat16


def halves(x):
    hi = x.astype(BF16)
    return hi, (x - hi.astype(F32)).astype(BF16)


def product(a_hi, a_lo, b_hi, b_lo):
    dot = functools.partial(jnp.dot, preferred_element_type=F32)
    return dot(a_hi, b_hi) + dot(a_hi, b_lo) + dot(a_lo, b_hi)


def kernel(
    cells,
    groups,
    trial,
    precond,
    dims,
    source,
    target,
    count,
    left_ops,
    right_ops,
    out,
    ritz,
    vec,
    vec_hi,
    vec_lo,
    part,
    in_f1,
    in_fd,
    in_f2,
    in_g,
    base,
    slope,
    last_theta,
    stage_l,
    stage_r,
    left_hi,
    left_lo,
    right_hi,
    right_lo,
    inner_hi,
    inner_lo,
    own_sums,
    term_sums,
    group_sums,
    sector_sums,
    ag_send,
    ag_recv,
    rs_send,
    f1_recv,
    fd_recv,
    f2_recv,
    g_recv,
    sum_send,
    sum_recv,
    load_sem,
):
    n_y, n_c = groups
    y, core = lax.axis_index("sector_0"), lax.axis_index("sector_1")
    x, z = lax.axis_index("term_0"), lax.axis_index("term_1")
    slots = left_hi.shape[0]
    width = left_hi.shape[1]
    coords = ((x, z), (z, x))
    names = (("term_0", "term_1"), ("term_1", "term_0"))

    def up(a, by):
        return lax.rem(a + by, 4)

    def unit(c, dp, dq):
        p, q = coords[c]
        return up(p, dp) * 4 + up(q, dq)

    def beside(c, axis, way):
        return {names[c][axis]: up(coords[c][axis], 1 if way == 0 else 3)}

    def load(k, which):
        src, dst = ((right_ops, stage_r), (left_ops, stage_l))[which]
        return pltpu.make_async_copy(src.at[k], dst.at[k], load_sem.at[which, k])

    for which in range(2):
        for k in range(slots):
            load(k, which).start()

    barrier = pltpu.get_barrier_semaphore()
    for d in range(1, 16):
        there = lax.rem(x * 4 + z + d, 16)
        pl.semaphore_signal(
            barrier, inc=1, device_id={"term_0": there // 4, "term_1": lax.rem(there, 4)}, device_id_type=MESH
        )
    n_groups = n_y * n_c
    for d in range(1, n_groups):
        there = lax.rem(y * n_c + core + d, n_groups)
        pl.semaphore_signal(
            barrier, inc=1, device_id={"sector_0": there // n_c, "sector_1": lax.rem(there, n_c)}, device_id_type=MESH
        )

    def prepare(which):
        stage, hi, lo = ((stage_r, right_hi, right_lo), (stage_l, left_hi, left_lo))[which]
        for k in range(slots):
            load(k, which).wait()

        def body(i, carry):
            k = i // 8
            rows = pl.ds(pl.multiple_of(lax.rem(i, 8) * (width // 8), width // 8), width // 8)
            hi[k, rows], lo[k, rows] = halves(stage[k, rows])
            return carry

        lax.fori_loop(0, slots * 8, body, 0)

    def mask(c, s):
        row = (x * 4 + z) * 32 + c * 16 + lax.broadcasted_iota(jnp.int32, (16, width), 0)
        col = lax.broadcasted_iota(jnp.int32, (16, width), 1)
        return (row < dims[s]) & (col < dims[s])

    for c in range(2):
        for s in range(2):
            vec[c, unit(c, 0, 0), s] = jnp.where(mask(c, s), trial[s, c * 16 : (c + 1) * 16], 0.0)

    pl.semaphore_wait(barrier, 15 + n_groups - 1)

    def remote(src, dst, send, recv, where):
        return pltpu.make_async_remote_copy(
            src_ref=src, dst_ref=dst, send_sem=send, recv_sem=recv, device_id=where, device_id_type=MESH
        )

    def away(c, axis, by):
        return {names[c][axis]: up(coords[c][axis], by)}

    MOVE = (1, 3, 2)

    def ag_row(c, way, at):
        ref = vec.at[c, at]
        return remote(ref, ref, ag_send, ag_recv.at[c, 0, way], away(c, 1, MOVE[way]))

    def ag_full(c, dq, way, at):
        ref = vec.at[c, at]
        return remote(ref, ref, ag_send, ag_recv.at[c, 1 + dq, way], away(c, 0, MOVE[way]))

    def ag_half(c, dq, way, at):
        ref = vec.at[c, at, way]
        return remote(ref, ref, ag_send, ag_recv.at[c, 1 + dq, 2 + way], away(c, 0, MOVE[way]))

    def came(way):
        return (3, 1, 2)[way]

    def lane_sums(value):
        folded = jnp.sum(value.reshape(-1, width), axis=0, keepdims=True)
        total = folded[:, 0:128]
        for i in range(1, width // 128):
            total = total + folded[:, i * 128 : (i + 1) * 128]
        return total

    def squares():
        total = jnp.zeros((1, 128), F32)
        for c in range(2):
            value = vec[c, unit(c, 0, 0)]
            total = total + lane_sums(value * value)
        return total

    def term_start(step):
        for d in range(1, 16):
            there = lax.rem(x * 4 + z + d, 16)
            remote(
                own_sums.at[step],
                term_sums.at[step, x * 4 + z],
                sum_send.at[step, 0],
                sum_recv.at[step, 0],
                {"term_0": there // 4, "term_1": lax.rem(there, 4)},
            ).start()
        term_sums[step, x * 4 + z] = own_sums[step]

    def wait_bytes(ref, sem):
        pltpu.make_async_copy(ref, ref, sem).wait()

    def sector_start(step):
        wait_bytes(term_sums.at[step, 0:15], sum_recv.at[step, 0])
        group_sums[step] = jnp.sum(term_sums[step], axis=0)
        me = y * n_c + core
        for d in range(1, n_groups):
            there = lax.rem(me + d, n_groups)
            remote(
                group_sums.at[step],
                sector_sums.at[step, me],
                sum_send.at[step, 1],
                sum_recv.at[step, 1],
                {"sector_0": there // n_c, "sector_1": lax.rem(there, n_c)},
            ).start()
        sector_sums[step, me] = group_sums[step]

    def sums_end(step):
        if n_groups > 1:
            wait_bytes(sector_sums.at[step, 0 : n_groups - 1], sum_recv.at[step, 1])
        total = jnp.sum(jnp.sum(sector_sums[step], axis=0), axis=1, keepdims=True)
        wait_bytes(term_sums.at[step, 0:15], sum_send.at[step, 0])
        if n_groups > 1:
            wait_bytes(sector_sums.at[step, 0 : n_groups - 1], sum_send.at[step, 1])
        return total

    def spot(c, dp, dq):
        p, q = up(coords[c][0], dp), up(coords[c][1], dq)
        row = (p * 128 + q * 32) if c == 0 else (q * 128 + p * 32 + 16)
        return c, p * 4 + q, pl.multiple_of(row, 16)

    def spots(group):
        return [spot(c, dp, dq) for c in range(2) for dp, dq in group]

    def first_products(group):
        places = spots(group)
        for c, at, _ in places:
            hi, lo = halves(vec[c, at])
            for s in range(2):
                vec_hi[s, c, at], vec_lo[s, c, at] = hi[s], lo[s]

        for k in range(slots):
            s = source[k]
            a_hi = jnp.concatenate([vec_hi[s, c, at] for c, at, _ in places], axis=0)
            a_lo = jnp.concatenate([vec_lo[s, c, at] for c, at, _ in places], axis=0)
            hi, lo = halves(product(a_hi, a_lo, right_hi[k], right_lo[k]))
            for i, (_, _, row) in enumerate(places):
                inner_hi[k, pl.ds(row, 16)] = hi[i * 16 : (i + 1) * 16]
                inner_lo[k, pl.ds(row, 16)] = lo[i * 16 : (i + 1) * 16]

    def second_products(group):
        places = spots(group)
        for k in range(slots):
            a_hi = jnp.concatenate([left_hi[k, pl.ds(row, 16)] for _, _, row in places], axis=0)
            a_lo = jnp.concatenate([left_lo[k, pl.ds(row, 16)] for _, _, row in places], axis=0)
            value = product(a_hi, a_lo, inner_hi[k], inner_lo[k])
            live = jnp.where(k < count[0], 1.0, 0.0).astype(F32)
            to_one = live * target[k].astype(F32)
            scale = (live - to_one, to_one)
            for i, (c, at, _) in enumerate(places):
                piece = value[i * 16 : (i + 1) * 16]
                for s in range(2):
                    old = part[c, at, s] if k else 0.0
                    part[c, at, s] = old + scale[s] * piece
        total = jnp.zeros((1, 128), F32)
        for c, at, _ in places:
            total = total + lane_sums(vec[c, at] * part[c, at])
        return total

    def f1(c, dq, way):
        return remote(
            part.at[c, unit(c, 2, dq), way], in_f1.at[c, dq, way], rs_send, f1_recv.at[c, dq, way], beside(c, 0, way)
        )

    def fd(c):
        return remote(part.at[c, unit(c, 2, 2)], in_fd.at[c], rs_send, fd_recv.at[c], away(c, 0, 2))

    def f2(c, dq, way):
        return remote(
            part.at[c, unit(c, MOVE[way], dq)], in_f2.at[c, dq, way], rs_send, f2_recv.at[c, dq, way], beside(c, 0, way)
        )

    def g(c, way):
        return remote(
            part.at[c, unit(c, 0, MOVE[way])], in_g.at[c, way], rs_send, g_recv.at[c, way], away(c, 1, MOVE[way])
        )

    def one_step(step, carry):
        for c in range(2):
            for way in range(2):
                ag_row(c, way, unit(c, 0, 0)).start()
        for c in range(2):
            for way in range(2):
                ag_full(c, 0, way, unit(c, 0, 0)).start()
        for c in range(2):
            ag_row(c, 2, unit(c, 0, 0)).start()
        @pl.when(step == 0)
        def _():
            prepare(0)

        own_sums[step, 1:2] = squares()
        for c in range(2):
            for way in range(2):
                dq = came(way)
                at = unit(c, 0, dq)
                ag_row(c, way, at).wait_recv()
                for w in range(2):
                    ag_full(c, dq, w, at).start()
        for c in range(2):
            for way in range(2):
                at = unit(c, came(way), 0)
                ag_full(c, 0, way, at).wait_recv()
                ag_half(c, 0, way, at).start()
        for c in range(2):
            at = unit(c, 0, 2)
            ag_row(c, 2, at).wait_recv()
            for w in range(3):
                ag_full(c, 2, w, at).start()
        first_products(((0, 0), (0, 1), (0, 3), (1, 0)))

        @pl.when(step == 0)
        def _():
            prepare(1)

        for dq in (3, 1):
            for c in range(2):
                for way in range(2):
                    at = unit(c, came(way), dq)
                    ag_full(c, dq, way, at).wait_recv()
                    ag_half(c, dq, way, at).start()
        first_products(((3, 0), (0, 2), (1, 1), (1, 3)))
        for c in range(2):
            for way in range(2):
                ag_half(c, 0, way, unit(c, 2, 0)).wait_recv()
                ag_full(c, 2, way, unit(c, came(way), 2)).wait_recv()
        first_products(((3, 1), (3, 3), (2, 0), (1, 2)))
        for c in range(2):
            ag_full(c, 2, 2, unit(c, 2, 2)).wait_recv()
            for dq in (1, 3):
                for way in range(2):
                    ag_half(c, dq, way, unit(c, 2, dq)).wait_recv()
        first_products(((3, 2), (2, 2), (2, 1), (2, 3)))
        wait_bytes(vec.at[0, 0:15], ag_send)
        wait_bytes(vec.at[1, 0:15], ag_send)

        total = second_products(((2, 0), (2, 1), (2, 2), (2, 3)))
        for dq in (1, 3):
            for c in range(2):
                for way in range(2):
                    f1(c, dq, way).start()
        for c in range(2):
            fd(c).start()
        for c in range(2):
            for way in range(2):
                f1(c, 0, way).start()
        total = total + second_products(((1, 2), (3, 2), (1, 1), (3, 1)))
        for c in range(2):
            for way in range(2):
                f2(c, 2, way).start()
        total = total + second_products(((1, 3), (3, 3), (1, 0), (3, 0)))

        def pass_on(c, dq, way):
            f1(c, dq, way).wait_recv()
            at = unit(c, MOVE[way], dq)
            part[c, at, way] = part[c, at, way] + in_f1[c, dq, way]
            f2(c, dq, way).start()

        for dq in (1, 3):
            for c in range(2):
                for way in range(2):
                    pass_on(c, dq, way)
        total = total + second_products(((0, 0), (0, 1), (0, 2), (0, 3)))
        own_sums[step, 0:1] = total
        own_sums[step, 2:3] = jnp.zeros((1, 128), F32)
        term_start(step)

        def take(c, dq):
            at = unit(c, 0, dq)
            for way in range(2):
                f2(c, dq, way).wait_recv()
            extra = in_f2[c, dq, 0] + in_f2[c, dq, 1]
            if dq == 2:
                fd(c).wait_recv()
                extra = extra + in_fd[c]
            part[c, at] = part[c, at] + extra

        for c in range(2):
            take(c, 2)
            g(c, 2).start()
        for c in range(2):
            for way in range(2):
                pass_on(c, 0, way)
        for way in range(2):
            for c in range(2):
                take(c, MOVE[way])
                g(c, way).start()
        sector_start(step)
        for c in range(2):
            take(c, 0)
        for c in range(2):
            for way in range(3):
                g(c, way).wait_recv()
        for c in range(2):
            at = unit(c, 0, 0)
            for s in range(2):
                w = part[c, at, s] + ((in_g[c, 0, s] + in_g[c, 1, s]) + in_g[c, 2, s])
                w = jnp.where(mask(c, s), w, 0.0)
                v = vec[c, at, s]
                p = precond[s, c * 16 : (c + 1) * 16]
                base[c, s] = v - w / p
                slope[c, s] = v / p

        @pl.when(step == STEPS - 1)
        def _():
            a, b = base[...], slope[...]
            own_sums[STEPS, 0:1] = lane_sums(a * a)
            own_sums[STEPS, 1:2] = lane_sums(a * b)
            own_sums[STEPS, 2:3] = lane_sums(b * b)
            term_start(STEPS)

        sums = sums_end(step)
        theta = sums[0:1] / sums[1:2]
        ritz[step] = theta[0, 0]
        scale = jnp.sqrt(cells / sums[1:2])
        for c in range(2):
            vec[c, unit(c, 0, 0)] = (base[c] + theta * slope[c]) * scale
        last_theta[...] = theta
        wait_bytes(part.at[0, 0:15], rs_send)
        wait_bytes(part.at[1, 0:15], rs_send)
        return carry

    lax.fori_loop(0, STEPS, one_step, 0)
    sector_start(STEPS)
    final = sums_end(STEPS)
    theta = last_theta[...]
    norm = final[0:1] + theta * (2.0 * final[1:2] + theta * final[2:3])
    scale = jnp.sqrt(cells / norm)
    for c in range(2):
        for s in range(2):
            out[s, c * 16 : (c + 1) * 16] = (base[c, s] + theta * slope[c, s]) * scale


def handover(vector, quotients, out, ritz):
    out[...] = vector[...]
    for step in range(STEPS):
        ritz[step] = quotients[step]


def per_device(trial, precond, sector_dims, left_ops, right_ops, task_source, task_target, task_count):
    sec_dev, share, width = trial.shape
    groups = (lax.axis_size("sector_0"), lax.axis_size("sector_1"))
    n_groups = groups[0] * groups[1]
    cells = float(sec_dev * n_groups * width * width)
    vmem = pl.BlockSpec(memory_space=pltpu.VMEM)
    smem = pl.BlockSpec(memory_space=pltpu.SMEM)
    anywhere = pl.BlockSpec(memory_space=pl.ANY)
    dma = pltpu.SemaphoreType.DMA
    ops = (LIVE, width, width)
    refined, quotients = pl.pallas_call(
        functools.partial(kernel, cells, groups),
        out_shape=(
            jax.ShapeDtypeStruct(trial.shape, F32),
            jax.ShapeDtypeStruct((STEPS,), F32),
        ),
        in_specs=[vmem, vmem, smem, smem, smem, smem, anywhere, anywhere],
        out_specs=(vmem, smem),
        scratch_shapes=[
            pltpu.VMEM((2, 16, 2, 16, width), F32),
            pltpu.VMEM((2, 2, 16, 16, width), BF16),
            pltpu.VMEM((2, 2, 16, 16, width), BF16),
            pltpu.VMEM((2, 16, 2, 16, width), F32),
            pltpu.VMEM((2, 4, 2, 16, width), F32),
            pltpu.VMEM((2, 2, 16, width), F32),
            pltpu.VMEM((2, 4, 2, 2, 16, width), F32),
            pltpu.VMEM((2, 3, 2, 16, width), F32),
            pltpu.VMEM((2, 2, 16, width), F32),
            pltpu.VMEM((2, 2, 16, width), F32),
            pltpu.VMEM((1, 1), F32),
            pltpu.VMEM(ops, F32),
            pltpu.VMEM(ops, F32),
            pltpu.VMEM(ops, BF16),
            pltpu.VMEM(ops, BF16),
            pltpu.VMEM(ops, BF16),
            pltpu.VMEM(ops, BF16),
            pltpu.VMEM(ops, BF16),
            pltpu.VMEM(ops, BF16),
            pltpu.VMEM((STEPS + 1, 3, 128), F32),
            pltpu.VMEM((STEPS + 1, 16, 3, 128), F32),
            pltpu.VMEM((STEPS + 1, 3, 128), F32),
            pltpu.VMEM((STEPS + 1, n_groups, 3, 128), F32),
            dma,
            dma((2, 5, 4)),
            dma,
            dma((2, 4, 2)),
            dma((2,)),
            dma((2, 4, 2)),
            dma((2, 3)),
            dma((STEPS + 1, 2)),
            dma((STEPS + 1, 2)),
            dma((2, LIVE)),
        ],
        compiler_params=pltpu.CompilerParams(
            collective_id=0, has_side_effects=True, vmem_limit_bytes=60 * 1024 * 1024
        ),
    )(trial, precond, sector_dims, task_source, task_target, task_count, left_ops, right_ops)
    return pl.pallas_call(
        handover,
        out_shape=(jax.ShapeDtypeStruct(trial.shape, F32), jax.ShapeDtypeStruct((STEPS,), F32)),
        in_specs=[vmem, smem],
        out_specs=(vmem, smem),
    )(refined, quotients)


def solution(mesh):
    finer = Mesh(mesh.devices.reshape(4, 2, 4, 4), SECTOR_TERM)
    placed = (
        P(SECTOR, TERM, None),
        P(SECTOR, TERM, None),
        P(SECTOR),
        P(SECTOR_TERM, None, None),
        P(SECTOR_TERM, None, None),
        P(SECTOR_TERM),
        P(SECTOR_TERM),
        P(SECTOR_TERM),
    )
    return jax.shard_map(
        per_device,
        mesh=finer,
        in_specs=placed,
        out_specs=(P(SECTOR, TERM, None), P()),
        check_vma=False,
    )
```

```python
import functools

import jax
import jax.numpy as jnp
from jax import lax
from jax.experimental import pallas as pl
from jax.experimental.pallas import tpu as pltpu
from jax.sharding import Mesh
from jax.sharding import PartitionSpec as P

STEPS = 3
LIVE = 7
SECTOR = ("sector_0", "sector_1")
TERM = ("term_0", "term_1")
SECTOR_TERM = SECTOR + TERM
MESH = pl.DeviceIdType.MESH
F32 = jnp.float32
BF16 = jnp.bfloat16


def halves(x):
    hi = x.astype(BF16)
    return hi, (x - hi.astype(F32)).astype(BF16)


def product(a_hi, a_lo, b_hi, b_lo):
    dot = functools.partial(jnp.dot, preferred_element_type=F32)
    return dot(a_hi, b_hi) + dot(a_hi, b_lo) + dot(a_lo, b_hi)


def kernel(
    cells,
    groups,
    trial,
    precond,
    dims,
    source,
    target,
    count,
    left_ops,
    right_ops,
    out,
    ritz,
    vec,
    vec_hi,
    vec_lo,
    part,
    in_f1,
    in_fd,
    in_f2,
    in_g,
    base,
    slope,
    last_theta,
    stage_l,
    stage_r,
    left_hi,
    left_lo,
    right_hi,
    right_lo,
    inner_hi,
    inner_lo,
    own_sums,
    term_sums,
    column_sums,
    sector_sums,
    ag_send,
    ag_recv,
    rs_send,
    f1_recv,
    fd_recv,
    f2_recv,
    g_recv,
    sum_send,
    sum_recv,
    load_sem,
):
    n_y, n_c = groups
    y, core = lax.axis_index("sector_0"), lax.axis_index("sector_1")
    x, z = lax.axis_index("term_0"), lax.axis_index("term_1")
    slots = left_hi.shape[0]
    width = left_hi.shape[1]
    coords = ((x, z), (z, x))
    names = (("term_0", "term_1"), ("term_1", "term_0"))

    def up(a, by):
        return lax.rem(a + by, 4)

    def unit(c, dp, dq):
        p, q = coords[c]
        return up(p, dp) * 4 + up(q, dq)

    def beside(c, axis, way):
        return {names[c][axis]: up(coords[c][axis], 1 if way == 0 else 3)}

    def load(k, which):
        src, dst = ((right_ops, stage_r), (left_ops, stage_l))[which]
        return pltpu.make_async_copy(src.at[k], dst.at[k], load_sem.at[which, k])

    for which in range(2):
        for k in range(slots):
            load(k, which).start()

    barrier = pltpu.get_barrier_semaphore()
    for d in range(1, 16):
        there = lax.rem(x * 4 + z + d, 16)
        pl.semaphore_signal(
            barrier, inc=1, device_id={"term_0": there // 4, "term_1": lax.rem(there, 4)}, device_id_type=MESH
        )
    n_groups = n_y * n_c
    for d in range(1, n_groups):
        there = lax.rem(y * n_c + core + d, n_groups)
        pl.semaphore_signal(
            barrier, inc=1, device_id={"sector_0": there // n_c, "sector_1": lax.rem(there, n_c)}, device_id_type=MESH
        )

    def prepare(which):
        stage, hi, lo = ((stage_r, right_hi, right_lo), (stage_l, left_hi, left_lo))[which]
        for k in range(slots):
            load(k, which).wait()

        def body(i, carry):
            k = i // 8
            rows = pl.ds(pl.multiple_of(lax.rem(i, 8) * (width // 8), width // 8), width // 8)
            hi[k, rows], lo[k, rows] = halves(stage[k, rows])
            return carry

        lax.fori_loop(0, slots * 8, body, 0)

    def mask(c, s):
        row = (x * 4 + z) * 32 + c * 16 + lax.broadcasted_iota(jnp.int32, (16, width), 0)
        col = lax.broadcasted_iota(jnp.int32, (16, width), 1)
        return (row < dims[s]) & (col < dims[s])

    for c in range(2):
        for s in range(2):
            vec[c, unit(c, 0, 0), s] = jnp.where(mask(c, s), trial[s, c * 16 : (c + 1) * 16], 0.0)

    pl.semaphore_wait(barrier, 15 + n_groups - 1)

    def remote(src, dst, send, recv, where):
        return pltpu.make_async_remote_copy(
            src_ref=src, dst_ref=dst, send_sem=send, recv_sem=recv, device_id=where, device_id_type=MESH
        )

    def away(c, axis, by):
        return {names[c][axis]: up(coords[c][axis], by)}

    MOVE = (1, 3, 2)

    def ag_row(c, way, at):
        ref = vec.at[c, at]
        return remote(ref, ref, ag_send, ag_recv.at[c, 0, way], away(c, 1, MOVE[way]))

    def ag_full(c, dq, way, at):
        ref = vec.at[c, at]
        return remote(ref, ref, ag_send, ag_recv.at[c, 1 + dq, way], away(c, 0, MOVE[way]))

    def ag_half(c, dq, way, at):
        ref = vec.at[c, at, way]
        return remote(ref, ref, ag_send, ag_recv.at[c, 1 + dq, 2 + way], away(c, 0, MOVE[way]))

    def came(way):
        return (3, 1, 2)[way]

    def lane_sums(value):
        folded = jnp.sum(value.reshape(-1, width), axis=0, keepdims=True)
        total = folded[:, 0:128]
        for i in range(1, width // 128):
            total = total + folded[:, i * 128 : (i + 1) * 128]
        return total

    def squares():
        total = jnp.zeros((1, 128), F32)
        for c in range(2):
            value = vec[c, unit(c, 0, 0)]
            total = total + lane_sums(value * value)
        return total

    me_sector, me_term = y * n_c + core, x * 4 + z

    def sums_start(step):
        for d in range(1, n_groups):
            there = lax.rem(me_sector + d, n_groups)
            remote(
                own_sums.at[step],
                sector_sums.at[step, me_sector],
                sum_send.at[step, 0],
                sum_recv.at[step, 0],
                {"sector_0": there // n_c, "sector_1": lax.rem(there, n_c)},
            ).start()
        sector_sums[step, me_sector] = own_sums[step]

    def wait_bytes(ref, sem):
        pltpu.make_async_copy(ref, ref, sem).wait()

    def sums_middle(step):
        if n_groups > 1:
            wait_bytes(sector_sums.at[step, 0 : n_groups - 1], sum_recv.at[step, 0])
        column_sums[step] = jnp.sum(sector_sums[step], axis=0)
        for d in range(1, 16):
            there = lax.rem(me_term + d, 16)
            remote(
                column_sums.at[step],
                term_sums.at[step, me_term],
                sum_send.at[step, 1],
                sum_recv.at[step, 1],
                {"term_0": there // 4, "term_1": lax.rem(there, 4)},
            ).start()
        term_sums[step, me_term] = column_sums[step]

    def sums_end(step):
        wait_bytes(term_sums.at[step, 0:15], sum_recv.at[step, 1])
        total = jnp.sum(jnp.sum(term_sums[step], axis=0), axis=1, keepdims=True)
        if n_groups > 1:
            wait_bytes(sector_sums.at[step, 0 : n_groups - 1], sum_send.at[step, 0])
        wait_bytes(term_sums.at[step, 0:15], sum_send.at[step, 1])
        return total

    def spot(c, dp, dq):
        p, q = up(coords[c][0], dp), up(coords[c][1], dq)
        row = (p * 128 + q * 32) if c == 0 else (q * 128 + p * 32 + 16)
        return c, p * 4 + q, pl.multiple_of(row, 16)

    def spots(group):
        return [spot(c, dp, dq) for c in range(2) for dp, dq in group]

    def first_products(group):
        places = spots(group)
        for c, at, _ in places:
            hi, lo = halves(vec[c, at])
            for s in range(2):
                vec_hi[s, c, at], vec_lo[s, c, at] = hi[s], lo[s]

        for k in range(slots):
            s = source[k]
            a_hi = jnp.concatenate([vec_hi[s, c, at] for c, at, _ in places], axis=0)
            a_lo = jnp.concatenate([vec_lo[s, c, at] for c, at, _ in places], axis=0)
            hi, lo = halves(product(a_hi, a_lo, right_hi[k], right_lo[k]))
            for i, (_, _, row) in enumerate(places):
                inner_hi[k, pl.ds(row, 16)] = hi[i * 16 : (i + 1) * 16]
                inner_lo[k, pl.ds(row, 16)] = lo[i * 16 : (i + 1) * 16]

    def second_products(group):
        places = spots(group)
        for k in range(slots):
            a_hi = jnp.concatenate([left_hi[k, pl.ds(row, 16)] for _, _, row in places], axis=0)
            a_lo = jnp.concatenate([left_lo[k, pl.ds(row, 16)] for _, _, row in places], axis=0)
            value = product(a_hi, a_lo, inner_hi[k], inner_lo[k])
            live = jnp.where(k < count[0], 1.0, 0.0).astype(F32)
            to_one = live * target[k].astype(F32)
            scale = (live - to_one, to_one)
            for i, (c, at, _) in enumerate(places):
                piece = value[i * 16 : (i + 1) * 16]
                for s in range(2):
                    old = part[c, at, s] if k else 0.0
                    part[c, at, s] = old + scale[s] * piece
        total = jnp.zeros((1, 128), F32)
        for c, at, _ in places:
            total = total + lane_sums(vec[c, at] * part[c, at])
        return total

    def f1(c, dq, way):
        return remote(
            part.at[c, unit(c, 2, dq), way], in_f1.at[c, dq, way], rs_send, f1_recv.at[c, dq, way], beside(c, 0, way)
        )

    def fd(c):
        return remote(part.at[c, unit(c, 2, 2)], in_fd.at[c], rs_send, fd_recv.at[c], away(c, 0, 2))

    def f2(c, dq, way):
        return remote(
            part.at[c, unit(c, MOVE[way], dq)], in_f2.at[c, dq, way], rs_send, f2_recv.at[c, dq, way], beside(c, 0, way)
        )

    def g(c, way):
        return remote(
            part.at[c, unit(c, 0, MOVE[way])], in_g.at[c, way], rs_send, g_recv.at[c, way], away(c, 1, MOVE[way])
        )

    def one_step(step, carry):
        for c in range(2):
            for way in range(2):
                ag_row(c, way, unit(c, 0, 0)).start()
        for c in range(2):
            for way in range(2):
                ag_full(c, 0, way, unit(c, 0, 0)).start()
        for c in range(2):
            ag_row(c, 2, unit(c, 0, 0)).start()
        @pl.when(step == 0)
        def _():
            prepare(0)

        own_sums[step, 1:2] = squares()
        for c in range(2):
            for way in range(2):
                dq = came(way)
                at = unit(c, 0, dq)
                ag_row(c, way, at).wait_recv()
                for w in range(2):
                    ag_full(c, dq, w, at).start()
        for c in range(2):
            for way in range(2):
                at = unit(c, came(way), 0)
                ag_full(c, 0, way, at).wait_recv()
                ag_half(c, 0, way, at).start()
        for c in range(2):
            at = unit(c, 0, 2)
            ag_row(c, 2, at).wait_recv()
            for w in range(3):
                ag_full(c, 2, w, at).start()
        first_products(((0, 0), (0, 1), (0, 3), (1, 0)))

        @pl.when(step == 0)
        def _():
            prepare(1)

        for dq in (3, 1):
            for c in range(2):
                for way in range(2):
                    at = unit(c, came(way), dq)
                    ag_full(c, dq, way, at).wait_recv()
                    ag_half(c, dq, way, at).start()
        first_products(((3, 0), (0, 2), (1, 1), (1, 3)))
        for c in range(2):
            for way in range(2):
                ag_half(c, 0, way, unit(c, 2, 0)).wait_recv()
                ag_full(c, 2, way, unit(c, came(way), 2)).wait_recv()
        first_products(((3, 1), (3, 3), (2, 0), (1, 2)))
        for c in range(2):
            ag_full(c, 2, 2, unit(c, 2, 2)).wait_recv()
            for dq in (1, 3):
                for way in range(2):
                    ag_half(c, dq, way, unit(c, 2, dq)).wait_recv()
        first_products(((3, 2), (2, 2), (2, 1), (2, 3)))
        wait_bytes(vec.at[0, 0:15], ag_send)
        wait_bytes(vec.at[1, 0:15], ag_send)

        total = second_products(((2, 0), (2, 1), (2, 2), (2, 3)))
        for dq in (1, 3):
            for c in range(2):
                for way in range(2):
                    f1(c, dq, way).start()
        for c in range(2):
            fd(c).start()
        for c in range(2):
            for way in range(2):
                f1(c, 0, way).start()
        total = total + second_products(((1, 2), (3, 2), (1, 1), (3, 1)))
        for c in range(2):
            for way in range(2):
                f2(c, 2, way).start()
        total = total + second_products(((1, 3), (3, 3), (1, 0), (3, 0)))

        def pass_on(c, dq, way):
            f1(c, dq, way).wait_recv()
            at = unit(c, MOVE[way], dq)
            part[c, at, way] = part[c, at, way] + in_f1[c, dq, way]
            f2(c, dq, way).start()

        for dq in (1, 3):
            for c in range(2):
                for way in range(2):
                    pass_on(c, dq, way)
        total = total + second_products(((0, 0), (0, 1), (0, 2), (0, 3)))
        own_sums[step, 0:1] = total
        own_sums[step, 2:3] = jnp.zeros((1, 128), F32)
        sums_start(step)

        def take(c, dq):
            at = unit(c, 0, dq)
            for way in range(2):
                f2(c, dq, way).wait_recv()
            extra = in_f2[c, dq, 0] + in_f2[c, dq, 1]
            if dq == 2:
                fd(c).wait_recv()
                extra = extra + in_fd[c]
            part[c, at] = part[c, at] + extra

        for c in range(2):
            take(c, 2)
            g(c, 2).start()
        for c in range(2):
            for way in range(2):
                pass_on(c, 0, way)
        sums_middle(step)
        for way in range(2):
            for c in range(2):
                take(c, MOVE[way])
                g(c, way).start()
        for c in range(2):
            take(c, 0)
        for c in range(2):
            for way in range(3):
                g(c, way).wait_recv()
        for c in range(2):
            at = unit(c, 0, 0)
            for s in range(2):
                w = part[c, at, s] + ((in_g[c, 0, s] + in_g[c, 1, s]) + in_g[c, 2, s])
                w = jnp.where(mask(c, s), w, 0.0)
                v = vec[c, at, s]
                p = precond[s, c * 16 : (c + 1) * 16]
                base[c, s] = v - w / p
                slope[c, s] = v / p

        @pl.when(step == STEPS - 1)
        def _():
            a, b = base[...], slope[...]
            own_sums[STEPS, 0:1] = lane_sums(a * a)
            own_sums[STEPS, 1:2] = lane_sums(a * b)
            own_sums[STEPS, 2:3] = lane_sums(b * b)
            sums_start(STEPS)

        sums = sums_end(step)
        theta = sums[0:1] / sums[1:2]
        ritz[step] = theta[0, 0]
        scale = jnp.sqrt(cells / sums[1:2])
        for c in range(2):
            vec[c, unit(c, 0, 0)] = (base[c] + theta * slope[c]) * scale
        last_theta[...] = theta
        wait_bytes(part.at[0, 0:15], rs_send)
        wait_bytes(part.at[1, 0:15], rs_send)
        return carry

    lax.fori_loop(0, STEPS, one_step, 0)
    sums_middle(STEPS)
    final = sums_end(STEPS)
    theta = last_theta[...]
    norm = final[0:1] + theta * (2.0 * final[1:2] + theta * final[2:3])
    scale = jnp.sqrt(cells / norm)
    for c in range(2):
        for s in range(2):
            out[s, c * 16 : (c + 1) * 16] = (base[c, s] + theta * slope[c, s]) * scale


def handover(vector, quotients, out, ritz):
    out[...] = vector[...]
    for step in range(STEPS):
        ritz[step] = quotients[step]


def per_device(trial, precond, sector_dims, left_ops, right_ops, task_source, task_target, task_count):
    sec_dev, share, width = trial.shape
    groups = (lax.axis_size("sector_0"), lax.axis_size("sector_1"))
    n_groups = groups[0] * groups[1]
    cells = float(sec_dev * n_groups * width * width)
    vmem = pl.BlockSpec(memory_space=pltpu.VMEM)
    smem = pl.BlockSpec(memory_space=pltpu.SMEM)
    anywhere = pl.BlockSpec(memory_space=pl.ANY)
    dma = pltpu.SemaphoreType.DMA
    ops = (LIVE, width, width)
    refined, quotients = pl.pallas_call(
        functools.partial(kernel, cells, groups),
        out_shape=(
            jax.ShapeDtypeStruct(trial.shape, F32),
            jax.ShapeDtypeStruct((STEPS,), F32),
        ),
        in_specs=[vmem, vmem, smem, smem, smem, smem, anywhere, anywhere],
        out_specs=(vmem, smem),
        scratch_shapes=[
            pltpu.VMEM((2, 16, 2, 16, width), F32),
            pltpu.VMEM((2, 2, 16, 16, width), BF16),
            pltpu.VMEM((2, 2, 16, 16, width), BF16),
            pltpu.VMEM((2, 16, 2, 16, width), F32),
            pltpu.VMEM((2, 4, 2, 16, width), F32),
            pltpu.VMEM((2, 2, 16, width), F32),
            pltpu.VMEM((2, 4, 2, 2, 16, width), F32),
            pltpu.VMEM((2, 3, 2, 16, width), F32),
            pltpu.VMEM((2, 2, 16, width), F32),
            pltpu.VMEM((2, 2, 16, width), F32),
            pltpu.VMEM((1, 1), F32),
            pltpu.VMEM(ops, F32),
            pltpu.VMEM(ops, F32),
            pltpu.VMEM(ops, BF16),
            pltpu.VMEM(ops, BF16),
            pltpu.VMEM(ops, BF16),
            pltpu.VMEM(ops, BF16),
            pltpu.VMEM(ops, BF16),
            pltpu.VMEM(ops, BF16),
            pltpu.VMEM((STEPS + 1, 3, 128), F32),
            pltpu.VMEM((STEPS + 1, 16, 3, 128), F32),
            pltpu.VMEM((STEPS + 1, 3, 128), F32),
            pltpu.VMEM((STEPS + 1, n_groups, 3, 128), F32),
            dma,
            dma((2, 5, 4)),
            dma,
            dma((2, 4, 2)),
            dma((2,)),
            dma((2, 4, 2)),
            dma((2, 3)),
            dma((STEPS + 1, 2)),
            dma((STEPS + 1, 2)),
            dma((2, LIVE)),
        ],
        compiler_params=pltpu.CompilerParams(
            collective_id=0, has_side_effects=True, vmem_limit_bytes=60 * 1024 * 1024
        ),
    )(trial, precond, sector_dims, task_source, task_target, task_count, left_ops, right_ops)
    return pl.pallas_call(
        handover,
        out_shape=(jax.ShapeDtypeStruct(trial.shape, F32), jax.ShapeDtypeStruct((STEPS,), F32)),
        in_specs=[vmem, smem],
        out_specs=(vmem, smem),
    )(refined, quotients)


def solution(mesh):
    finer = Mesh(mesh.devices.reshape(4, 2, 4, 4), SECTOR_TERM)
    placed = (
        P(SECTOR, TERM, None),
        P(SECTOR, TERM, None),
        P(SECTOR),
        P(SECTOR_TERM, None, None),
        P(SECTOR_TERM, None, None),
        P(SECTOR_TERM),
        P(SECTOR_TERM),
        P(SECTOR_TERM),
    )
    return jax.shard_map(
        per_device,
        mesh=finer,
        in_specs=placed,
        out_specs=(P(SECTOR, TERM, None), P()),
        check_vma=False,
    )
```

```python
import functools

import jax
import jax.numpy as jnp
from jax import lax
from jax.experimental import pallas as pl
from jax.experimental.pallas import tpu as pltpu
from jax.sharding import Mesh
from jax.sharding import PartitionSpec as P

STEPS = 3
LIVE = 7
SECTOR = ("sector_0", "sector_1")
TERM = ("term_0", "term_1")
SECTOR_TERM = SECTOR + TERM
MESH = pl.DeviceIdType.MESH
F32 = jnp.float32
BF16 = jnp.bfloat16


def halves(x):
    hi = x.astype(BF16)
    return hi, (x - hi.astype(F32)).astype(BF16)


def product(a_hi, a_lo, b_hi, b_lo):
    dot = functools.partial(jnp.dot, preferred_element_type=F32)
    return dot(a_hi, b_hi) + dot(a_hi, b_lo) + dot(a_lo, b_hi)


def kernel(
    cells,
    groups,
    trial,
    precond,
    dims,
    source,
    target,
    count,
    left_ops,
    right_ops,
    out,
    ritz,
    vec,
    vec_hi,
    vec_lo,
    part,
    in_f1,
    in_fd,
    in_f2,
    in_g,
    base,
    slope,
    last_theta,
    stage_l,
    stage_r,
    left_hi,
    left_lo,
    right_hi,
    right_lo,
    inner_hi,
    inner_lo,
    own_sums,
    term_sums,
    column_sums,
    sector_sums,
    ag_send,
    ag_recv,
    rs_send,
    f1_recv,
    fd_recv,
    f2_recv,
    g_recv,
    sum_send,
    sum_recv,
    load_sem,
):
    n_y, n_c = groups
    y, core = lax.axis_index("sector_0"), lax.axis_index("sector_1")
    x, z = lax.axis_index("term_0"), lax.axis_index("term_1")
    slots = left_hi.shape[0]
    width = left_hi.shape[1]
    coords = ((x, z), (z, x))
    names = (("term_0", "term_1"), ("term_1", "term_0"))

    def up(a, by):
        return lax.rem(a + by, 4)

    def unit(c, dp, dq):
        p, q = coords[c]
        return up(p, dp) * 4 + up(q, dq)

    def beside(c, axis, way):
        return {names[c][axis]: up(coords[c][axis], 1 if way == 0 else 3)}

    def load(k, which):
        src, dst = ((right_ops, stage_r), (left_ops, stage_l))[which]
        return pltpu.make_async_copy(src.at[k], dst.at[k], load_sem.at[which, k])

    for which in range(2):
        for k in range(slots):
            load(k, which).start()

    barrier = pltpu.get_barrier_semaphore()
    for d in range(1, 16):
        there = lax.rem(x * 4 + z + d, 16)
        pl.semaphore_signal(
            barrier, inc=1, device_id={"term_0": there // 4, "term_1": lax.rem(there, 4)}, device_id_type=MESH
        )
    n_groups = n_y * n_c
    for d in range(1, n_groups):
        there = lax.rem(y * n_c + core + d, n_groups)
        pl.semaphore_signal(
            barrier, inc=1, device_id={"sector_0": there // n_c, "sector_1": lax.rem(there, n_c)}, device_id_type=MESH
        )

    def prepare(which):
        stage, hi, lo = ((stage_r, right_hi, right_lo), (stage_l, left_hi, left_lo))[which]
        for k in range(slots):
            load(k, which).wait()

        def body(i, carry):
            k = i // 8
            rows = pl.ds(pl.multiple_of(lax.rem(i, 8) * (width // 8), width // 8), width // 8)
            hi[k, rows], lo[k, rows] = halves(stage[k, rows])
            return carry

        lax.fori_loop(0, slots * 8, body, 0)

    def mask(c, s):
        row = (x * 4 + z) * 32 + c * 16 + lax.broadcasted_iota(jnp.int32, (16, width), 0)
        col = lax.broadcasted_iota(jnp.int32, (16, width), 1)
        return (row < dims[s]) & (col < dims[s])

    for c in range(2):
        for s in range(2):
            vec[c, unit(c, 0, 0), s] = jnp.where(mask(c, s), trial[s, c * 16 : (c + 1) * 16], 0.0)

    pl.semaphore_wait(barrier, 15 + n_groups - 1)

    def remote(src, dst, send, recv, where):
        return pltpu.make_async_remote_copy(
            src_ref=src, dst_ref=dst, send_sem=send, recv_sem=recv, device_id=where, device_id_type=MESH
        )

    def away(c, axis, by):
        return {names[c][axis]: up(coords[c][axis], by)}

    MOVE = (1, 3, 2)

    def ag_row(c, way, at):
        ref = vec.at[c, at]
        return remote(ref, ref, ag_send, ag_recv.at[c, 0, way], away(c, 1, MOVE[way]))

    def ag_full(c, dq, way, at):
        ref = vec.at[c, at]
        return remote(ref, ref, ag_send, ag_recv.at[c, 1 + dq, way], away(c, 0, MOVE[way]))

    def ag_half(c, dq, way, at):
        ref = vec.at[c, at, way]
        return remote(ref, ref, ag_send, ag_recv.at[c, 1 + dq, 2 + way], away(c, 0, MOVE[way]))

    def came(way):
        return (3, 1, 2)[way]

    def lane_sums(value):
        folded = jnp.sum(value.reshape(-1, width), axis=0, keepdims=True)
        total = folded[:, 0:128]
        for i in range(1, width // 128):
            total = total + folded[:, i * 128 : (i + 1) * 128]
        return total

    def squares():
        total = jnp.zeros((1, 128), F32)
        for c in range(2):
            value = vec[c, unit(c, 0, 0)]
            total = total + lane_sums(value * value)
        return total

    me_sector, me_term = y * n_c + core, x * 4 + z

    def sums_start(step):
        for d in range(1, n_groups):
            there = lax.rem(me_sector + d, n_groups)
            remote(
                own_sums.at[step],
                sector_sums.at[step, me_sector],
                sum_send.at[step, 0],
                sum_recv.at[step, 0],
                {"sector_0": there // n_c, "sector_1": lax.rem(there, n_c)},
            ).start()
        sector_sums[step, me_sector] = own_sums[step]

    def wait_bytes(ref, sem):
        pltpu.make_async_copy(ref, ref, sem).wait()

    def sums_middle(step):
        if n_groups > 1:
            wait_bytes(sector_sums.at[step, 0 : n_groups - 1], sum_recv.at[step, 0])
        column_sums[step] = jnp.sum(sector_sums[step], axis=0)
        for d in range(1, 16):
            there = lax.rem(me_term + d, 16)
            remote(
                column_sums.at[step],
                term_sums.at[step, me_term],
                sum_send.at[step, 1],
                sum_recv.at[step, 1],
                {"term_0": there // 4, "term_1": lax.rem(there, 4)},
            ).start()
        term_sums[step, me_term] = column_sums[step]

    def sums_end(step):
        wait_bytes(term_sums.at[step, 0:15], sum_recv.at[step, 1])
        total = jnp.sum(jnp.sum(term_sums[step], axis=0), axis=1, keepdims=True)
        if n_groups > 1:
            wait_bytes(sector_sums.at[step, 0 : n_groups - 1], sum_send.at[step, 0])
        wait_bytes(term_sums.at[step, 0:15], sum_send.at[step, 1])
        return total

    def spot(c, dp, dq):
        p, q = up(coords[c][0], dp), up(coords[c][1], dq)
        row = (p * 128 + q * 32) if c == 0 else (q * 128 + p * 32 + 16)
        return c, p * 4 + q, pl.multiple_of(row, 16)

    def spots(group):
        return [spot(c, dp, dq) for c in range(2) for dp, dq in group]

    def first_products(group):
        places = spots(group)
        for c, at, _ in places:
            hi, lo = halves(vec[c, at])
            for s in range(2):
                vec_hi[s, c, at], vec_lo[s, c, at] = hi[s], lo[s]

        for k in range(slots):
            s = source[k]
            a_hi = jnp.concatenate([vec_hi[s, c, at] for c, at, _ in places], axis=0)
            a_lo = jnp.concatenate([vec_lo[s, c, at] for c, at, _ in places], axis=0)
            hi, lo = halves(product(a_hi, a_lo, right_hi[k], right_lo[k]))
            for i, (_, _, row) in enumerate(places):
                inner_hi[k, pl.ds(row, 16)] = hi[i * 16 : (i + 1) * 16]
                inner_lo[k, pl.ds(row, 16)] = lo[i * 16 : (i + 1) * 16]

    def second_products(group):
        places = spots(group)
        for k in range(slots):
            a_hi = jnp.concatenate([left_hi[k, pl.ds(row, 16)] for _, _, row in places], axis=0)
            a_lo = jnp.concatenate([left_lo[k, pl.ds(row, 16)] for _, _, row in places], axis=0)
            value = product(a_hi, a_lo, inner_hi[k], inner_lo[k])
            live = jnp.where(k < count[0], 1.0, 0.0).astype(F32)
            to_one = live * target[k].astype(F32)
            scale = (live - to_one, to_one)
            for i, (c, at, _) in enumerate(places):
                piece = value[i * 16 : (i + 1) * 16]
                for s in range(2):
                    old = part[c, at, s] if k else 0.0
                    part[c, at, s] = old + scale[s] * piece
        total = jnp.zeros((1, 128), F32)
        for c, at, _ in places:
            total = total + lane_sums(vec[c, at] * part[c, at])
        return total

    def f1(c, dq, way):
        return remote(
            part.at[c, unit(c, 2, dq), way], in_f1.at[c, dq, way], rs_send, f1_recv.at[c, dq, way], beside(c, 0, way)
        )

    def fd(c):
        return remote(part.at[c, unit(c, 2, 2)], in_fd.at[c], rs_send, fd_recv.at[c], away(c, 0, 2))

    def f2(c, dq, way):
        return remote(
            part.at[c, unit(c, MOVE[way], dq)], in_f2.at[c, dq, way], rs_send, f2_recv.at[c, dq, way], beside(c, 0, way)
        )

    def g(c, way):
        return remote(
            part.at[c, unit(c, 0, MOVE[way])], in_g.at[c, way], rs_send, g_recv.at[c, way], away(c, 1, MOVE[way])
        )

    def one_step(step, carry):
        for c in range(2):
            for way in range(2):
                ag_row(c, way, unit(c, 0, 0)).start()
        for c in range(2):
            for way in range(2):
                ag_full(c, 0, way, unit(c, 0, 0)).start()
        for c in range(2):
            ag_row(c, 2, unit(c, 0, 0)).start()
        @pl.when(step == 0)
        def _():
            prepare(0)

        own_sums[step, 1:2] = squares()
        for c in range(2):
            for way in range(2):
                dq = came(way)
                at = unit(c, 0, dq)
                ag_row(c, way, at).wait_recv()
                for w in range(2):
                    ag_full(c, dq, w, at).start()
        for c in range(2):
            for way in range(2):
                at = unit(c, came(way), 0)
                ag_full(c, 0, way, at).wait_recv()
                ag_half(c, 0, way, at).start()
        for c in range(2):
            at = unit(c, 0, 2)
            ag_row(c, 2, at).wait_recv()
            for w in range(3):
                ag_full(c, 2, w, at).start()
        first_products(((0, 0), (0, 1), (0, 3), (1, 0)))

        @pl.when(step == 0)
        def _():
            prepare(1)

        for dq in (3, 1):
            for c in range(2):
                for way in range(2):
                    at = unit(c, came(way), dq)
                    ag_full(c, dq, way, at).wait_recv()
                    ag_half(c, dq, way, at).start()
        first_products(((3, 0), (0, 2), (1, 1), (1, 3)))
        for c in range(2):
            for way in range(2):
                ag_half(c, 0, way, unit(c, 2, 0)).wait_recv()
                ag_full(c, 2, way, unit(c, came(way), 2)).wait_recv()
        first_products(((3, 1), (3, 3), (2, 0), (1, 2)))
        for c in range(2):
            ag_full(c, 2, 2, unit(c, 2, 2)).wait_recv()
            for dq in (1, 3):
                for way in range(2):
                    ag_half(c, dq, way, unit(c, 2, dq)).wait_recv()
        first_products(((3, 2), (2, 2), (2, 1), (2, 3)))
        wait_bytes(vec.at[0, 0:15], ag_send)
        wait_bytes(vec.at[1, 0:15], ag_send)

        total = second_products(((2, 0), (2, 1), (2, 2), (2, 3)))
        for dq in (1, 3):
            for c in range(2):
                for way in range(2):
                    f1(c, dq, way).start()
        for c in range(2):
            fd(c).start()
        for c in range(2):
            for way in range(2):
                f1(c, 0, way).start()
        total = total + second_products(((1, 2), (3, 2), (1, 1), (3, 1)))
        for c in range(2):
            for way in range(2):
                f2(c, 2, way).start()
        total = total + second_products(((1, 3), (3, 3), (1, 0), (3, 0)))

        def pass_on(c, dq, way):
            f1(c, dq, way).wait_recv()
            at = unit(c, MOVE[way], dq)
            part[c, at, way] = part[c, at, way] + in_f1[c, dq, way]
            f2(c, dq, way).start()

        total = total + second_products(((0, 0), (0, 1), (0, 2), (0, 3)))
        own_sums[step, 0:1] = total
        own_sums[step, 2:3] = jnp.zeros((1, 128), F32)
        sums_start(step)
        for dq in (1, 3):
            for c in range(2):
                for way in range(2):
                    pass_on(c, dq, way)

        def take(c, dq):
            at = unit(c, 0, dq)
            for way in range(2):
                f2(c, dq, way).wait_recv()
            extra = in_f2[c, dq, 0] + in_f2[c, dq, 1]
            if dq == 2:
                fd(c).wait_recv()
                extra = extra + in_fd[c]
            part[c, at] = part[c, at] + extra

        for c in range(2):
            take(c, 2)
            g(c, 2).start()
        for c in range(2):
            for way in range(2):
                pass_on(c, 0, way)
        sums_middle(step)
        for way in range(2):
            for c in range(2):
                take(c, MOVE[way])
                g(c, way).start()
        for c in range(2):
            take(c, 0)
        for c in range(2):
            for way in range(3):
                g(c, way).wait_recv()
        for c in range(2):
            at = unit(c, 0, 0)
            for s in range(2):
                w = part[c, at, s] + ((in_g[c, 0, s] + in_g[c, 1, s]) + in_g[c, 2, s])
                w = jnp.where(mask(c, s), w, 0.0)
                v = vec[c, at, s]
                p = precond[s, c * 16 : (c + 1) * 16]
                base[c, s] = v - w / p
                slope[c, s] = v / p

        @pl.when(step == STEPS - 1)
        def _():
            a, b = base[...], slope[...]
            own_sums[STEPS, 0:1] = lane_sums(a * a)
            own_sums[STEPS, 1:2] = lane_sums(a * b)
            own_sums[STEPS, 2:3] = lane_sums(b * b)
            sums_start(STEPS)

        sums = sums_end(step)
        theta = sums[0:1] / sums[1:2]
        ritz[step] = theta[0, 0]
        scale = jnp.sqrt(cells / sums[1:2])
        for c in range(2):
            vec[c, unit(c, 0, 0)] = (base[c] + theta * slope[c]) * scale
        last_theta[...] = theta
        wait_bytes(part.at[0, 0:15], rs_send)
        wait_bytes(part.at[1, 0:15], rs_send)
        return carry

    lax.fori_loop(0, STEPS, one_step, 0)
    sums_middle(STEPS)
    final = sums_end(STEPS)
    theta = last_theta[...]
    norm = final[0:1] + theta * (2.0 * final[1:2] + theta * final[2:3])
    scale = jnp.sqrt(cells / norm)
    for c in range(2):
        for s in range(2):
            out[s, c * 16 : (c + 1) * 16] = (base[c, s] + theta * slope[c, s]) * scale


def handover(vector, quotients, out, ritz):
    out[...] = vector[...]
    for step in range(STEPS):
        ritz[step] = quotients[step]


def per_device(trial, precond, sector_dims, left_ops, right_ops, task_source, task_target, task_count):
    sec_dev, share, width = trial.shape
    groups = (lax.axis_size("sector_0"), lax.axis_size("sector_1"))
    n_groups = groups[0] * groups[1]
    cells = float(sec_dev * n_groups * width * width)
    vmem = pl.BlockSpec(memory_space=pltpu.VMEM)
    smem = pl.BlockSpec(memory_space=pltpu.SMEM)
    anywhere = pl.BlockSpec(memory_space=pl.ANY)
    dma = pltpu.SemaphoreType.DMA
    ops = (LIVE, width, width)
    refined, quotients = pl.pallas_call(
        functools.partial(kernel, cells, groups),
        out_shape=(
            jax.ShapeDtypeStruct(trial.shape, F32),
            jax.ShapeDtypeStruct((STEPS,), F32),
        ),
        in_specs=[vmem, vmem, smem, smem, smem, smem, anywhere, anywhere],
        out_specs=(vmem, smem),
        scratch_shapes=[
            pltpu.VMEM((2, 16, 2, 16, width), F32),
            pltpu.VMEM((2, 2, 16, 16, width), BF16),
            pltpu.VMEM((2, 2, 16, 16, width), BF16),
            pltpu.VMEM((2, 16, 2, 16, width), F32),
            pltpu.VMEM((2, 4, 2, 16, width), F32),
            pltpu.VMEM((2, 2, 16, width), F32),
            pltpu.VMEM((2, 4, 2, 2, 16, width), F32),
            pltpu.VMEM((2, 3, 2, 16, width), F32),
            pltpu.VMEM((2, 2, 16, width), F32),
            pltpu.VMEM((2, 2, 16, width), F32),
            pltpu.VMEM((1, 1), F32),
            pltpu.VMEM(ops, F32),
            pltpu.VMEM(ops, F32),
            pltpu.VMEM(ops, BF16),
            pltpu.VMEM(ops, BF16),
            pltpu.VMEM(ops, BF16),
            pltpu.VMEM(ops, BF16),
            pltpu.VMEM(ops, BF16),
            pltpu.VMEM(ops, BF16),
            pltpu.VMEM((STEPS + 1, 3, 128), F32),
            pltpu.VMEM((STEPS + 1, 16, 3, 128), F32),
            pltpu.VMEM((STEPS + 1, 3, 128), F32),
            pltpu.VMEM((STEPS + 1, n_groups, 3, 128), F32),
            dma,
            dma((2, 5, 4)),
            dma,
            dma((2, 4, 2)),
            dma((2,)),
            dma((2, 4, 2)),
            dma((2, 3)),
            dma((STEPS + 1, 2)),
            dma((STEPS + 1, 2)),
            dma((2, LIVE)),
        ],
        compiler_params=pltpu.CompilerParams(
            collective_id=0, has_side_effects=True, vmem_limit_bytes=60 * 1024 * 1024
        ),
    )(trial, precond, sector_dims, task_source, task_target, task_count, left_ops, right_ops)
    return pl.pallas_call(
        handover,
        out_shape=(jax.ShapeDtypeStruct(trial.shape, F32), jax.ShapeDtypeStruct((STEPS,), F32)),
        in_specs=[vmem, smem],
        out_specs=(vmem, smem),
    )(refined, quotients)


def solution(mesh):
    finer = Mesh(mesh.devices.reshape(4, 2, 4, 4), SECTOR_TERM)
    placed = (
        P(SECTOR, TERM, None),
        P(SECTOR, TERM, None),
        P(SECTOR),
        P(SECTOR_TERM, None, None),
        P(SECTOR_TERM, None, None),
        P(SECTOR_TERM),
        P(SECTOR_TERM),
        P(SECTOR_TERM),
    )
    return jax.shard_map(
        per_device,
        mesh=finer,
        in_specs=placed,
        out_specs=(P(SECTOR, TERM, None), P()),
        check_vma=False,
    )
```
